256 devices in a mesh: gz: 8 (over y, core), gx: 8 (over x, z_lo), gy: 4 (over z_hi).
Axes of the slice: x: 4, y: 4, z: 8 (z_hi: 4, z_lo: 2; z = z_hi * 2 + z_lo), core: 2. Of those that a mesh axis runs over, the one named last changes fastest.
Arguments:
- initial_field: float32 [16, 1024, 512], P('gz', 'gx', 'gy'), may hold values from -6 to 6
- source_term: float32 [16, 1024, 512], P('gz', 'gx', 'gy'), may hold values from -48 to 48
- block_inverse: float32 [1024, 512, 128], P('gx', 'gy'), may hold values from -0.1 to 0.1
Outputs:
- smoothed: float32 [16, 1024, 512], P('gz', 'gx', 'gy')
The draws below stay inside these ranges and needn't reach their ends.
All inputs are finite; a program needn't handle non-finite values.
Results may differ from the reference program's by a relative error of at most 0.00013.
Values sent between devices are 32-bit elements; how exact they have to be, the bound alone decides.
A program may use at most 64 MiB of HBM per device.

```python
import math
import jax
import jax.numpy as jnp
from jax import lax

LINE = 128
NZ = 16
NX = 1024
NY = 512


def smooth_wave(key, grid_shape, first_axis, first_count, second_axis, second_count):
    phases = jax.random.uniform(key, (2,), jnp.float32, -math.pi, math.pi)
    first_pos = lax.broadcasted_iota(jnp.float32, grid_shape, first_axis) * (2.0 * math.pi / first_count)
    second_pos = lax.broadcasted_iota(jnp.float32, grid_shape, second_axis) * (2.0 * math.pi / second_count)
    return jnp.cos(first_pos + phases[0]) * jnp.cos(second_pos + phases[1])


def draw_initial_field(key, part):
    wave_key, noise_key = jax.random.split(jax.random.fold_in(key, 21))
    grid_shape = (NZ, NX, NY)
    wave_part = smooth_wave(wave_key, grid_shape, 1, NX, 0, NZ)
    smooth_part = -2.0 * (1.0 + 0.4 * wave_part)
    noise_part = jnp.clip(jax.random.normal(noise_key, grid_shape, jnp.float32), -3.0, 3.0)
    return (smooth_part + noise_part).astype(jnp.float32)


def draw_source_term(key, part):
    wave_key, noise_key = jax.random.split(jax.random.fold_in(key, 31))
    grid_shape = (NZ, NX, NY)
    wave_part = smooth_wave(wave_key, grid_shape, 1, NX, 2, NY)
    smooth_part = 10.0 * (1.0 + 0.5 * wave_part)
    noise_part = jnp.clip(8.0 * jax.random.normal(noise_key, grid_shape, jnp.float32), -30.0, 30.0)
    return (smooth_part + noise_part).astype(jnp.float32)


def draw_block_inverse(key, part):
    first_key, second_key = jax.random.split(jax.random.fold_in(key, 11))
    row_index = lax.broadcasted_iota(jnp.int32, (NX, NY, LINE), 1) % LINE
    col_index = lax.broadcasted_iota(jnp.int32, (NX, NY, LINE), 2)
    strength = jnp.exp(jax.random.uniform(first_key, (NX, NY, 1), jnp.float32, math.log(1.2), math.log(1.9)))
    spread = jnp.clip(jax.random.normal(second_key, (NX, NY, LINE), jnp.float32), -5.0, 5.0)
    diagonal_part = jnp.where(row_index == col_index, strength, 0.0)
    off_part = spread * (0.4 / math.sqrt(LINE))
    return ((diagonal_part + off_part) / 26.0).astype(jnp.float32)


def setup_inputs(seed: int = 0) -> dict:
    arg_keys = jax.random.split(jax.random.key(seed), 4)
    return {
        "initial_field": draw_initial_field(jax.random.fold_in(arg_keys[3], 71), 0),
        "source_term": draw_source_term(jax.random.fold_in(arg_keys[3], 71), 0),
        "block_inverse": draw_block_inverse(jax.random.fold_in(arg_keys[3], 71), 0),
    }


exact_mode = lax.Precision.HIGHEST


def box_sum(plane):
    padded = jnp.pad(plane, 1)
    row_sums = padded[:-2] + padded[1:-1] + padded[2:]
    return row_sums[:, :-2] + row_sums[:, 1:-1] + row_sums[:, 2:]


def apply_blocks(block_inverse, residual):
    count_x, count_y = residual.shape
    width = block_inverse.shape[2]
    lines = residual.reshape(count_x, count_y // width, width)
    blocks = block_inverse.reshape(count_x, count_y // width, width, width)
    return jnp.einsum("xqij,xqj->xqi", blocks, lines, precision=exact_mode).reshape(count_x, count_y)


def sweep_planes(field_now, source_term, block_inverse, backward):
    padded = jnp.pad(field_now, ((1, 1), (0, 0), (0, 0)))

    def update_plane(step, padded):
        if backward:
            zindex = (NZ - 1 - step).astype(jnp.int32)
        else:
            zindex = jnp.asarray(step).astype(jnp.int32)
        triple = lax.dynamic_slice_in_dim(padded, zindex, 3, 0)
        neighbours = box_sum(triple[0]) + box_sum(triple[1]) + box_sum(triple[2])
        source_plane = lax.dynamic_index_in_dim(source_term, zindex, 0, keepdims=False)
        residual = source_plane - (27.0 * triple[1] - neighbours)
        fresh = triple[1] + apply_blocks(block_inverse, residual)
        return lax.dynamic_update_slice_in_dim(padded, fresh[None], zindex + 1, 0)

    padded = lax.fori_loop(0, NZ, update_plane, padded)
    return padded[1:-1]


def reference(initial_field, source_term, block_inverse):
    forward = sweep_planes(initial_field, source_term, block_inverse, False)
    return sweep_planes(forward, source_term, block_inverse, True)
```

```python
import jax
import jax.numpy as jnp
from jax import lax
from jax.experimental import pallas as pl
from jax.experimental.pallas import tpu as pltpu
from jax.sharding import PartitionSpec as P

MESH = pl.DeviceIdType.MESH
NZ = 16
OWN = 16
HALO = 8
WIN = OWN + 2 * HALO
GROUPS = 4
STEPS = 4
ROUNDS = 2 * NZ // STEPS
GZ, GX, GY = 8, 8, 4
TAPS = tuple((lag, off) for lag in (1, 2, 3) for off in range(1 - lag, lag))
TAP_ROWS = 40


def lane_roll(x, amount):
    return x if amount % 128 == 0 else pltpu.roll(x, amount % 128, axis=1)


def box_x(x):
    return x + lane_roll(x, 1) + lane_roll(x, -1)


def lane_group(shape):
    return lax.broadcasted_iota(jnp.int32, shape, 1) // WIN


def unpack(packed):
    group = lane_group(packed.shape)
    turned = [lane_roll(packed, WIN * m) for m in range(GROUPS)]
    parts = []
    for h in range(GROUPS):
        part = turned[3]
        for m in (2, 1, 0):
            part = jnp.where(group == (h + m) % GROUPS, turned[m], part)
        parts.append(part)
    return jnp.concatenate(parts, axis=0)


def pack(field):
    rows = field.shape[0] // GROUPS
    group = lane_group((rows, 128))
    out = field[3 * rows :]
    for h in (2, 1, 0):
        out = jnp.where(group == h, field[h * rows : (h + 1) * rows], out)
    return out


def row_sums(accs):
    sub = lax.broadcasted_iota(jnp.int32, (8, 128), 0)
    for dist in (4, 2, 1):
        low = (sub // dist) % 2 == 0
        accs = [
            jnp.where(
                low,
                accs[k] + pltpu.roll(accs[k], 8 - dist, axis=0),
                accs[k + dist] + pltpu.roll(accs[k + dist], dist, axis=0),
            )
            for k in range(dist)
        ]
    return accs[0]


def swap_edges(edges):
    row = lax.broadcasted_iota(jnp.int32, (8, 128), 0)
    swapped = jnp.where(row % 2 == 0, pltpu.roll(edges, 1, axis=0), pltpu.roll(edges, 7, axis=0))
    swapped = jnp.where((row == 0) | (row == 7), 0.0, swapped)
    return box_x(swapped)


def swap_sides(x):
    row = lax.broadcasted_iota(jnp.int32, (8, 128), 0)
    return jnp.where(row % 2 == 0, pltpu.roll(x, 7, axis=0), pltpu.roll(x, 1, axis=0))


def kernel(
    v_ref, s_ref, a_ref, o_ref,
    aw, a2, win_v, win_s, field, source, base, edge, prev, shift, inject,
    phi_out, phi_in, phi, ve_out, ve_in, g_out, g_in, taps, cols, rows_t,
    xs, xr, xs_last, xr_last, g_stage, out_buf,
    al_sem, ar_send, ar_recv, w_send, w_recv, wx_send, wx_recv,
    phi_send, phi_recv, ve_send, ve_recv, g_send, g_recv,
    x_send, x_recv, f_send, f_recv,
):
    iz, ix, iy = lax.axis_index("gz"), lax.axis_index("gx"), lax.axis_index("gy")
    even = 1 - ix % 2
    p = even * iz + (1 - even) * (7 - iz)
    first, last = 1 - (p + 7) // 8, p // 7
    sign = 2 * even - 1
    lz, lx = iz - sign * (1 - first), ix - first
    rz, rx = iz + sign * (1 - last), ix + last
    has_left, has_right = lx >= 0, rx < GX
    cross_left, cross_right = (p == 0) & (ix > 0), (p == 7) & (ix < GX - 1)
    next_first, prev_last = 7 * even, 7 * (1 - even)

    def dev(z, x, y):
        return {"gz": z, "gx": x, "gy": y}

    def remote(src, dst, send, recv, target):
        return pltpu.make_async_remote_copy(
            src_ref=src, dst_ref=dst, send_sem=send, recv_sem=recv, device_id=target, device_id_type=MESH
        )

    a_mid = pltpu.make_async_copy(a_ref.at[pl.ds(16 * p, 16)], aw.at[pl.ds(8, 16)], al_sem.at[0])
    a_mid.start()

    def a_low():
        return pltpu.make_async_copy(a_ref.at[pl.ds(16 * p - 8, 8)], aw.at[pl.ds(0, 8)], al_sem.at[1])

    def a_high():
        return pltpu.make_async_copy(a_ref.at[pl.ds(16 * p + 16, 8)], aw.at[pl.ds(24, 8)], al_sem.at[2])

    @pl.when(p > 0)
    def _():
        a_low().start()

    @pl.when(p < 7)
    def _():
        a_high().start()

    @pl.when(jnp.logical_not(has_left))
    def _():
        aw[0:8] = jnp.zeros((8, 128, 128), jnp.float32)
        win_v[:, 0:8] = jnp.zeros((NZ, 8, 128), jnp.float32)
        win_s[:, 0:8] = jnp.zeros((NZ, 8, 128), jnp.float32)
        xr[0] = jnp.zeros(xr.shape[1:], jnp.float32)
        xr_last[0] = jnp.zeros(xr_last.shape[1:], jnp.float32)

    @pl.when(jnp.logical_not(has_right))
    def _():
        aw[24:32] = jnp.zeros((8, 128, 128), jnp.float32)
        win_v[:, 24:32] = jnp.zeros((NZ, 8, 128), jnp.float32)
        win_s[:, 24:32] = jnp.zeros((NZ, 8, 128), jnp.float32)
        xr[1] = jnp.zeros(xr.shape[1:], jnp.float32)
        xr_last[1] = jnp.zeros(xr_last.shape[1:], jnp.float32)

    barrier = pltpu.get_barrier_semaphore()

    def greet(z, x, y):
        pl.semaphore_signal(barrier, inc=1, device_id=dev(z, x, y), device_id_type=MESH)

    for k in range(1, GZ):
        greet((iz + k) % GZ, ix, iy)
    for k in range(1, GY):
        greet(iz, ix, (iy + k) % GY)

    @pl.when(ix < GX - 1)
    def _():
        greet(next_first, ix + 1, iy)

    @pl.when(ix > 0)
    def _():
        greet(prev_last, ix - 1, iy)

    @pl.when(cross_left)
    def _():
        for z in range(GZ):
            greet(z, ix - 1, iy)

    @pl.when(cross_right)
    def _():
        for z in range(GZ):
            greet(z, ix + 1, iy)

    more_left, more_right = (ix + 7) // 8, 1 - ix // 7
    pl.semaphore_wait(
        barrier,
        (GZ - 1) + (GY - 1) + more_left + more_right + 8 * first * more_left + 8 * last * more_right,
    )

    def window_copies(src_rows, dst_rows, count, kind, slot, owner, target, send, recv):
        made = []
        for n, (plane_ref, window) in enumerate(((v_ref, win_v), (s_ref, win_s))):
            made.append(
                remote(
                    plane_ref.at[:, pl.ds(src_rows, count)],
                    window.at[pl.ds(2 * owner, 2), pl.ds(dst_rows, count)],
                    send.at[n, kind, slot],
                    recv.at[n, kind, owner],
                    target,
                )
            )
        return made

    def mates(action):
        for k in range(1, GZ):
            z = (iz + k) % GZ
            pz = even * z + (1 - even) * (7 - z)
            target = dev(z, ix, iy)
            action(window_copies(16 * pz, 8, 16, 0, k, iz, target, w_send, w_recv))

            @pl.when(pz > 0)
            def _():
                action(window_copies(16 * pz - 8, 0, 8, 1, k, iz, target, w_send, w_recv))

            @pl.when(pz < 7)
            def _():
                action(window_copies(16 * pz + 16, 24, 8, 2, k, iz, target, w_send, w_recv))

        @pl.when(ix < GX - 1)
        def _():
            action(window_copies(120, 0, 8, 0, 0, iz, dev(next_first, ix + 1, iy), wx_send, wx_recv))

        @pl.when(ix > 0)
        def _():
            action(window_copies(0, 24, 8, 1, 0, iz, dev(prev_last, ix - 1, iy), wx_send, wx_recv))

    def start_all(copies):
        for copy in copies:
            copy.start()

    def sent_all(copies):
        for copy in copies:
            copy.wait_send()

    def got_all(copies):
        for copy in copies:
            copy.wait_recv()

    mates(start_all)

    def a_right():
        return remote(a_ref.at[pl.ds(120, 8)], aw.at[pl.ds(0, 8)], ar_send.at[0], ar_recv.at[0], dev(iz, ix + 1, iy))

    def a_left():
        return remote(a_ref.at[pl.ds(0, 8)], aw.at[pl.ds(24, 8)], ar_send.at[1], ar_recv.at[1], dev(iz, ix - 1, iy))

    @pl.when(cross_right)
    def _():
        a_right().start()

    @pl.when(cross_left)
    def _():
        a_left().start()

    for plane_ref, window in ((v_ref, win_v), (s_ref, win_s)):
        window[pl.ds(2 * iz, 2), 8:24] = plane_ref[:, pl.ds(pl.multiple_of(16 * p, 8), 16)]

        @pl.when(p > 0)
        def _():
            window[pl.ds(2 * iz, 2), 0:8] = plane_ref[:, pl.ds(pl.multiple_of(16 * p - 8, 8), 8)]

        @pl.when(p < 7)
        def _():
            window[pl.ds(2 * iz, 2), 24:32] = plane_ref[:, pl.ds(pl.multiple_of(16 * p + 16, 8), 8)]

    for k in range(1, GZ):
        z = (iz + k) % GZ
        me = dev((iz + 1) % GZ, ix, iy)
        got_all(window_copies(0, 8, 16, 0, k, z, me, w_send, w_recv))

        @pl.when(p > 0)
        def _():
            got_all(window_copies(0, 0, 8, 1, k, z, me, w_send, w_recv))

        @pl.when(p < 7)
        def _():
            got_all(window_copies(0, 24, 8, 2, k, z, me, w_send, w_recv))

    @pl.when(cross_left)
    def _():
        for z in range(GZ):
            got_all(window_copies(0, 0, 8, 0, 0, z, dev(iz, ix - 1, iy), wx_send, wx_recv))

    @pl.when(cross_right)
    def _():
        for z in range(GZ):
            got_all(window_copies(0, 24, 8, 1, 0, z, dev(iz, ix + 1, iy), wx_send, wx_recv))

    zero_plane = jnp.zeros((128, 128), jnp.float32)
    field[0] = zero_plane
    field[NZ + 1] = zero_plane
    edge[0] = jnp.zeros((8, 128), jnp.float32)
    edge[NZ + 1] = jnp.zeros((8, 128), jnp.float32)

    def turn_plane(z, c):
        w = win_v[z]
        field[z + 1] = jnp.concatenate([w] * GROUPS, axis=0).T
        w = win_s[z]
        source[z] = jnp.concatenate([w] * GROUPS, axis=0).T
        return c

    lax.fori_loop(0, NZ, turn_plane, 0)
    for z in range(NZ):
        ve_out[2 * z : 2 * z + 1] = field[z + 1, 0:1]
        ve_out[2 * z + 1 : 2 * z + 2] = field[z + 1, 127:128]

    def to_blocks(src, dst, send, recv, k):
        return remote(src, dst.at[iy], send.at[k], recv.at[iy], dev(iz, ix, (iy + k) % GY))

    def from_blocks(src, dst, send, recv, k):
        y = (iy + k) % GY
        return remote(src, dst.at[y], send.at[k], recv.at[y], dev(iz, ix, y))

    for k in range(1, GY):
        to_blocks(ve_out, ve_in, ve_send, ve_recv, k).start()
    ve_in[iy] = ve_out[...]

    a_mid.wait()

    @pl.when(p > 0)
    def _():
        a_low().wait()

    @pl.when(p < 7)
    def _():
        a_high().wait()

    @pl.when(cross_left)
    def _():
        a_right().wait_recv()

    @pl.when(cross_right)
    def _():
        a_left().wait_recv()

    def turn_block(i_lo, c):
        parts = [aw[:, pl.ds(h * WIN + i_lo, 1), :].reshape(WIN, 128) for h in range(GROUPS)]
        a2[i_lo] = jnp.concatenate(parts, axis=0).T
        return c

    lax.fori_loop(0, WIN, turn_block, 0)

    def block_product(residual):
        out = []
        for b in range(4):
            accs = []
            for k in range(8):
                acc = a2[8 * b + k, 0:8] * residual[0:8]
                for m in range(1, 16):
                    acc = acc + a2[8 * b + k, 8 * m : 8 * m + 8] * residual[8 * m : 8 * m + 8]
                accs.append(acc)
            out.append(row_sums(accs))
        return unpack(jnp.concatenate(out, axis=0))

    def sum_y(x, low, high):
        shift[8:136] = x
        shift[7:8] = low
        shift[136:137] = high
        return shift[7:135] + x + shift[9:137]

    zero_row = jnp.zeros((1, 128), jnp.float32)

    ends = (0, 127)
    for n, end in enumerate(ends):
        cols[n] = unpack(jnp.concatenate([a2[i, end : end + 1] for i in range(WIN)], axis=0))
        row = a2[end % WIN]
        group = lane_group((128, 128))
        out = row
        for m in range(1, GROUPS):
            out = jnp.where(group == (end // WIN + m) % GROUPS, lane_roll(row, WIN * m), out)
        rows_t[n] = sum_y(out, zero_row, zero_row)
    for side in range(2):
        for n in range(2):
            first_tap = 2 * (side != n) + side
            g_out[first_tap : first_tap + 1] = cols[n, ends[side] : ends[side] + 1]

    def second(index, c):
        n, off = index // 3, index % 3 - 1
        col = cols[n]
        shifted = jnp.where(off == 0, col, jnp.where(off > 0, lane_roll(col, -1), lane_roll(col, 1)))
        cols[2 + index] = block_product(sum_y(shifted, zero_row, zero_row))
        return c

    lax.fori_loop(0, 6, second, 0)
    third = {}
    for n in range(2):
        for off in (-1, 0, 1):
            col = cols[2 + 3 * n + off + 1]
            tap = TAPS.index((2, off))
            for side in range(2):
                at = 4 * tap + 2 * (side != n) + side
                g_out[at : at + 1] = col[ends[side] : ends[side] + 1]
                row = rows_t[side]
                for step in (-1, 0, 1):
                    part = jnp.sum(lane_roll(row, step) * col, axis=0, keepdims=True)
                    part = lane_roll(jnp.broadcast_to(part, (8, 128)), -step)
                    key = (n, side, step + off)
                    third[key] = part if key not in third else third[key] + part
    for (n, side, off), part in third.items():
        at = 4 * TAPS.index((3, off)) + 2 * (side != n) + side
        g_out[at : at + 1] = part[0:1]
    g_out[36:40] = jnp.zeros((4, 128), jnp.float32)
    for k in range(1, GY):
        to_blocks(g_out, g_in, g_send, g_recv, k).start()
    g_in[iy] = g_out[...]

    for k in range(1, GY):
        from_blocks(ve_out, ve_in, ve_send, ve_recv, k).wait_recv()
    for z in range(NZ):
        for y in range(GY):
            edge[z + 1, 2 * y : 2 * y + 2] = ve_in[y, 2 * z : 2 * z + 2]

    def plane_at(rr, j):
        t = STEPS * rr + j
        forward = 1 - rr // (ROUNDS // 2)
        return forward * t + (1 - forward) * (2 * NZ - 1 - t), 2 * forward - 1

    def set_base(rr):
        def one(j, c):
            z, ahead = plane_at(rr, j)
            centre = field[z + 1]
            edges = swap_edges(edge[z + 1] + edge[z + 1 + ahead])
            inject[5] = edges
            low = inject[5, pl.ds(2 * iy, 1)]
            high = inject[5, pl.ds(2 * iy + 1, 1)]
            both = sum_y(box_x(centre + field[z + 1 + ahead]), low, high)
            base[z] = source[z] - (27.0 * centre - both)
            return c

        lax.fori_loop(0, STEPS, one, 0)

    def advance(z, slot):
        low = inject[slot, pl.ds(2 * iy, 1)]
        high = inject[slot, pl.ds(2 * iy + 1, 1)]
        residual = base[z] + sum_y(box_x(prev[...]), low, high)
        return field[z + 1] + block_product(residual)

    def x_copies(rr):
        out = []
        for side, (z, x) in enumerate(((rz, rx), (lz, lx))):
            for n, (start, count) in enumerate(((STEPS * rr + 3, 1), (STEPS * rr, 3))):
                rows = pl.ds(start, count)
                out.append(
                    remote(
                        xs.at[rows], xr.at[side, rows],
                        x_send.at[side, n, rr], x_recv.at[side, n, rr], dev(z, x, iy),
                    )
                )
        return out

    def last_copies():
        return [
            remote(xs_last, xr_last.at[side], x_send.at[side, 0, 4], x_recv.at[side, 0, 4], dev(z, x, iy))
            for side, (z, x) in enumerate(((rz, rx), (lz, lx)))
        ]

    def when_sides(make, pick, to_do, sending):
        @pl.when(has_right if sending else has_left)
        def _():
            copies = make()
            to_do([copies[n] for n in pick(len(copies), 0)])

        @pl.when(has_left if sending else has_right)
        def _():
            copies = make()
            to_do([copies[n] for n in pick(len(copies), 1)])

    def pick_all(count, side):
        return range(side * count // 2, (side + 1) * count // 2)

    def pick_first(count, side):
        return range(side * count // 2, side * count // 2 + 1)

    def pick_rest(count, side):
        return range(side * count // 2 + 1, (side + 1) * count // 2)

    def merged(own, left, right):
        x = lax.broadcasted_iota(jnp.int32, own.shape, 1) % WIN
        return jnp.where(x < HALO, lane_roll(left, -OWN), jnp.where(x >= HALO + OWN, lane_roll(right, OWN), own))

    def emit(rr):
        for pair in range(2):
            m = (2 * NZ - 1 - STEPS * rr) // 2 - pair
            for n in range(2):
                g_stage[2 * m + n] = field[2 * m + n + 1].T[HALO : HALO + OWN]

            @pl.when(m == iz)
            def _():
                out_buf[:, pl.ds(pl.multiple_of(16 * p, 8), 16)] = g_stage[pl.ds(2 * iz, 2)]

            @pl.when(m != iz)
            def _():
                out_copy(m).start()

    def out_copy(m):
        return remote(
            g_stage.at[pl.ds(2 * m, 2)],
            out_buf.at[:, pl.ds(16 * p, 16)],
            f_send.at[m],
            f_recv.at[iz],
            dev(m, ix, iy),
        )

    zero_tile = jnp.zeros((8, 128), jnp.float32)
    inject[0] = zero_tile
    inject[4] = zero_tile
    prev[...] = zero_plane
    set_base(0)

    def one_round(rr, c):
        slot = rr % 2

        def free(j, c):
            z, _ = plane_at(rr, j)
            fresh = advance(z, 4 * ((j + 3) // 4))
            prev[...] = fresh
            phi_out[slot, pl.ds(2 * j, 1)] = fresh[0:1]
            phi_out[slot, pl.ds(2 * j + 1, 1)] = fresh[127:128]

            @pl.when(j == 0)
            def _():
                field[z + 1] = fresh

            return c

        lax.fori_loop(0, STEPS, free, 0)
        for k in range(1, GY):
            to_blocks(phi_out.at[slot], phi_in.at[slot], phi_send.at[slot], phi_recv.at[slot], k).start()
        phi_in[slot, iy] = phi_out[slot]

        z0, _ = plane_at(rr, 0)
        prev[...] = field[z0 + 1]

        @pl.when((rr != ROUNDS // 2 - 1) & (rr < ROUNDS - 1))
        def _():
            set_base(rr + 1)

        @pl.when(rr > ROUNDS // 2)
        def _():
            emit(rr - 1)

        @pl.when(rr == 0)
        def _():
            for k in range(1, GY):
                from_blocks(g_out, g_in, g_send, g_recv, k).wait_recv()
            for tap in range(len(TAPS)):
                for kind in range(2):
                    for y in range(GY):
                        at = 4 * tap + 2 * kind
                        taps[tap, kind, 2 * y : 2 * y + 2] = g_in[y, at : at + 2]

        for k in range(1, GY):
            from_blocks(phi_out.at[slot], phi_in.at[slot], phi_send.at[slot], phi_recv.at[slot], k).wait()
        for j in range(STEPS):
            for y in range(GY):
                phi[j, 2 * y : 2 * y + 2] = phi_in[slot, y, 2 * j : 2 * j + 2]
        injected = []
        for j in range(STEPS):
            edges = phi[j]
            for lag in range(1, j + 1):
                straight, crossed = injected[j - lag]
                for off in range(1 - lag, lag):
                    tap = TAPS.index((lag, off))
                    edges = edges + taps[tap, 0] * lane_roll(straight, -off) + taps[tap, 1] * lane_roll(crossed, -off)
            z, _ = plane_at(rr, j)
            edge[z + 1] = edges
            straight = swap_edges(edges)
            injected.append((straight, swap_sides(straight)))
            inject[(j + 1) % STEPS] = straight

        def true(j, c):
            z, _ = plane_at(rr, j)
            fresh = advance(z, j)
            prev[...] = fresh
            field[z + 1] = fresh
            return c

        lax.fori_loop(1, STEPS, true, 0)

        @pl.when(rr < ROUNDS // 2)
        def _():
            for j in range(STEPS):
                z = STEPS * rr + j
                xs[z, 0:32] = pack(field[z + 1])
                xs[z, 32:40] = edge[z + 1]
            when_sides(lambda: x_copies(rr), pick_all, start_all, True)

        @pl.when(rr == 1)
        def _():
            when_sides(lambda: x_copies(rr), pick_first, got_all, False)
            z = 2 * STEPS - 1
            fresh = unpack(merged(xs[z, 0:32], xr[0, z, 0:32], xr[1, z, 0:32]))
            prev[...] = fresh
            inject[0] = swap_edges(merged(xs[z, 32:40], xr[0, z, 32:40], xr[1, z, 32:40]))

        @pl.when(rr == 3)
        def _():
            for r in (0, 2, 3):
                when_sides(lambda: x_copies(r), pick_first, got_all, False)
            for r in range(4):
                when_sides(lambda: x_copies(r), pick_rest, got_all, False)

            def one(z, c):
                field[z + 1] = unpack(merged(xs[z, 0:32], xr[0, z, 0:32], xr[1, z, 0:32]))
                edge[z + 1] = merged(xs[z, 32:40], xr[0, z, 32:40], xr[1, z, 32:40])
                return c

            lax.fori_loop(0, NZ, one, 0)
            prev[...] = zero_plane
            inject[0] = zero_tile
            set_base(ROUNDS // 2)

        @pl.when(rr == 5)
        def _():
            xs_last[0:32] = pack(prev[...])
            xs_last[32:40] = edge[NZ // 2 + 1]
            when_sides(last_copies, pick_all, start_all, True)
            when_sides(last_copies, pick_all, got_all, False)
            prev[...] = unpack(merged(xs_last[0:32], xr_last[0, 0:32], xr_last[1, 0:32]))
            inject[0] = swap_edges(merged(xs_last[32:40], xr_last[0, 32:40], xr_last[1, 32:40]))

        return c

    lax.fori_loop(0, ROUNDS, one_round, 0)
    emit(ROUNDS - 1)

    mates(sent_all)

    @pl.when(cross_right)
    def _():
        a_right().wait_send()

    @pl.when(cross_left)
    def _():
        a_left().wait_send()

    for k in range(1, GY):
        to_blocks(ve_out, ve_in, ve_send, ve_recv, k).wait_send()
        to_blocks(g_out, g_in, g_send, g_recv, k).wait_send()
    for r in range(4):
        when_sides(lambda: x_copies(r), pick_all, sent_all, True)
    when_sides(last_copies, pick_all, sent_all, True)
    for k in range(1, GZ):
        z = (iz + k) % GZ
        out_copy(z).wait_send()
        remote(
            g_stage.at[pl.ds(0, 2)], out_buf.at[:, pl.ds(0, 16)], f_send.at[z], f_recv.at[z], dev(z, ix, iy)
        ).wait_recv()
    o_ref[...] = out_buf[...]


def body(initial_field, source_term, block_inverse):
    f32 = jnp.float32
    dma = pltpu.SemaphoreType.DMA
    vmem = pltpu.VMEM
    return pl.pallas_call(
        kernel,
        out_shape=jax.ShapeDtypeStruct(initial_field.shape, f32),
        in_specs=[
            pl.BlockSpec(memory_space=pltpu.VMEM),
            pl.BlockSpec(memory_space=pltpu.VMEM),
            pl.BlockSpec(memory_space=pl.ANY),
        ],
        out_specs=pl.BlockSpec(memory_space=pltpu.VMEM),
        scratch_shapes=[
            vmem((WIN, 128, 128), f32),
            vmem((WIN, 128, 128), f32),
            vmem((NZ, WIN, 128), f32),
            vmem((NZ, WIN, 128), f32),
            vmem((NZ + 2, 128, 128), f32),
            vmem((NZ, 128, 128), f32),
            vmem((NZ, 128, 128), f32),
            vmem((NZ + 2, 8, 128), f32),
            vmem((128, 128), f32),
            vmem((144, 128), f32),
            vmem((6, 8, 128), f32),
            vmem((2, 8, 128), f32),
            vmem((2, GY, 8, 128), f32),
            vmem((STEPS, 8, 128), f32),
            vmem((2 * NZ, 128), f32),
            vmem((GY, 2 * NZ, 128), f32),
            vmem((TAP_ROWS, 128), f32),
            vmem((GY, TAP_ROWS, 128), f32),
            vmem((len(TAPS), 2, 8, 128), f32),
            vmem((8, 128, 128), f32),
            vmem((2, 128, 128), f32),
            vmem((NZ, 40, 128), f32),
            vmem((2, NZ, 40, 128), f32),
            vmem((40, 128), f32),
            vmem((2, 40, 128), f32),
            vmem((NZ, OWN, 128), f32),
            vmem((2, 128, 128), f32),
            dma((3,)),
            dma((2,)),
            dma((2,)),
            dma((2, 3, GZ)),
            dma((2, 3, GZ)),
            dma((2, 2, 1)),
            dma((2, 2, GZ)),
            dma((2, GY)),
            dma((2, GY)),
            dma((GY,)),
            dma((GY,)),
            dma((GY,)),
            dma((GY,)),
            dma((2, 2, 5)),
            dma((2, 2, 5)),
            dma((GZ,)),
            dma((GZ,)),
        ],
        compiler_params=pltpu.CompilerParams(collective_id=0, has_side_effects=True),
    )(initial_field, source_term, block_inverse)


def solution(mesh):
    placed = (P("gz", "gx", "gy"), P("gz", "gx", "gy"), P("gx", "gy", None))
    return jax.shard_map(
        body, mesh=mesh, in_specs=placed, out_specs=P("gz", "gx", "gy"), check_vma=False
    )
```
